512 devices in a mesh: row: 16 (over x_lo, z), vec: 32 (over y, x_hi, core).
Axes of the slice: x: 4 (x_hi: 2, x_lo: 2; x = x_hi * 2 + x_lo), y: 8, z: 8, core: 2. Of those that a mesh axis runs over, the one named last changes fastest.
Arguments:
- vectors: float32 [16384, 16384], P('row', 'vec'), may hold values from -6 to 6
- block_index: int32 [3, 16], replicated, may hold values from 0 to 31
- block_offset: int32 [3, 16], replicated, may hold values from 0 to 3, as said below
- reflector_vectors: float32 [16, 32, 512, 256], P('row', 'vec'), may hold values from -0.25 to 0.25
- reflector_factors: float32 [16, 32, 256, 256], P('row', 'vec'), may hold values from -0.1875 to 0.1875
Outputs:
- updated: float32 [16384, 16384], P('row', 'vec')
The draws below stay inside these ranges and needn't reach their ends.
Inputs may be any that keep to these rules, and one draw needn't show every extreme that they name: `block_offset`: the last owner's offset is at most 2, so every block lies inside the slab.
All inputs are finite; a program needn't handle non-finite values.
Results may differ from the reference program's by a relative error of at most 0.0001.
Values sent between devices are 32-bit elements; how exact they have to be, the bound alone decides.
A program may use at most 64 MiB of HBM per device.

```python
import jax
import jax.numpy as jnp
from jax import lax

ROW_DEV = 1024
REFL = 256
BLOCK_ROWS = 512
FRONTS = 3
NR = 16384
NV = 16384
POOL = 32
N_ROW = 16
N_VEC = 32


def draw_block_offset(key, part):
    slots = ROW_DEV // REFL
    first_key, second_key = jax.random.split(jax.random.fold_in(key, 11))
    base = jax.random.randint(first_key, (FRONTS, N_ROW), 0, slots)
    upper = jax.random.randint(second_key, (FRONTS, N_ROW), 0, 2)
    value = jnp.where(upper == 1, slots - 1, base)
    final = jnp.arange(N_ROW) == N_ROW - 1
    return jnp.where(final[None, :], jnp.minimum(value, slots - 2), value).astype(jnp.int32)


def place_ends(values, own_key, low, largest):
    longest = values.shape.index(max(values.shape))
    spots = []
    for shift in (0, 1):
        where = [jax.random.randint(jax.random.fold_in(own_key, axis), (), 0, length) for axis, length in enumerate(values.shape)]
        where[longest] = (where[longest] + shift) % values.shape[longest]
        spots.append(tuple(where))
    return values.at[spots[0]].set(low).at[spots[1]].set(largest)


def levels(rng, shape, pieces, low, high):
    loudness, own = 1.0, jax.random.fold_in(rng, 6)
    for axis_at, parts in pieces:
        draws = jnp.exp(jax.random.uniform(jax.random.fold_in(own, axis_at), (parts,), jnp.float32, low / len(pieces), high / len(pieces)))
        loudness = loudness * jnp.repeat(draws, shape[axis_at] // parts).reshape([-1 if axis == axis_at else 1 for axis in range(len(shape))])
    return loudness


def centred(own_key, dims, deviation, most, cuts=(), kind=jnp.bfloat16):
    result = deviation * jax.random.normal(own_key, dims, jnp.float32)
    if cuts:
        result = result * levels(own_key, dims, cuts, -0.22, 0.18)
    return jnp.clip(result, -most, most).astype(kind)


def setup_inputs(seed: int = 0) -> dict:
    arg_keys = jax.random.split(jax.random.key(seed), 6)
    vectors = centred(arg_keys[0], (NR, NV), 1.0, 6.0, ((0, 16), (1, 32)), jnp.float32)
    block_index = place_ends(jax.random.randint(arg_keys[1], (FRONTS, N_ROW), 0, N_VEC), jax.random.fold_in(arg_keys[1], 1), 0, N_VEC - 1).astype(jnp.int32)
    block_offset = draw_block_offset(jax.random.fold_in(arg_keys[5], 71), 0)
    reflector_vectors = centred(arg_keys[3], (N_ROW, POOL, BLOCK_ROWS, REFL), BLOCK_ROWS ** -0.5, 0.25, ((0, 16), (1, 32)), jnp.float32)
    reflector_factors = centred(arg_keys[4], (N_ROW, POOL, REFL, REFL), (4 * REFL) ** -0.5, 0.1875, ((0, 16), (1, 32)), jnp.float32)
    return {"vectors": vectors, "block_index": block_index, "block_offset": block_offset, "reflector_vectors": reflector_vectors, "reflector_factors": reflector_factors}


def apply_reflector_block(row_window, vector_matrix, triangular_matrix):
    high_precision = lax.Precision.HIGHEST
    inner_product = jnp.dot(vector_matrix.T, row_window, precision=high_precision, preferred_element_type=jnp.float32)
    mixed_rows = jnp.dot(jnp.triu(triangular_matrix), inner_product, precision=high_precision, preferred_element_type=jnp.float32)
    return row_window - jnp.dot(vector_matrix, mixed_rows, precision=high_precision, preferred_element_type=jnp.float32)


def reference(vectors, block_index, block_offset, reflector_vectors, reflector_factors):
    def one_block(step, row_slab):
        front = step // N_ROW
        owner_index = step % N_ROW
        select_block = block_index[front, owner_index]
        vector_matrix = reflector_vectors[owner_index, select_block]
        triangular_matrix = reflector_factors[owner_index, select_block]
        start_row = (owner_index * ROW_DEV + block_offset[front, owner_index] * REFL).astype(jnp.int32)
        row_window = lax.dynamic_slice_in_dim(row_slab, start_row, BLOCK_ROWS, 0)
        return lax.dynamic_update_slice_in_dim(row_slab, apply_reflector_block(row_window, vector_matrix, triangular_matrix), start_row, 0)

    return lax.fori_loop(0, FRONTS * N_ROW, one_block, vectors)
```

```python
import functools

import jax
import jax.numpy as jnp
from jax import lax
from jax.experimental import pallas as pl
from jax.experimental.pallas import tpu as pltpu
from jax.sharding import PartitionSpec as P

MESH = pl.DeviceIdType.MESH
F32, BF16 = jnp.float32, jnp.bfloat16
FRONTS = 3
R = 256
H = 128
PACK = 704
NC = 4


def split(x):
    high = x.astype(BF16)
    return high, (x - high.astype(F32)).astype(BF16)


def where(value, target, yes, no):
    return jnp.where(jnp.full(yes.shape, value, jnp.int32) == jnp.full(yes.shape, target, jnp.int32), yes, no)


def mm(a, b):
    dot = functools.partial(jnp.dot, preferred_element_type=F32)
    return dot(a[0], b[0]) + (dot(a[0], b[1]) + dot(a[1], b[0]))


def kernel(
    n_row,
    n_vec,
    slab,
    index,
    offset,
    v_hbm,
    s_hbm,
    out,
    w,
    first,
    din,
    uout,
    uin,
    dout,
    pad,
    blk,
    sib_blk,
    vb,
    ps,
    pr,
    ms,
    mr,
    xs,
    xr,
    vt_h,
    vt_l,
    v_h,
    v_l,
    sx_h,
    sx_l,
    so_h,
    so_l,
    in_sem,
    raw_sem,
    p_ssem,
    p_rsem,
    m_ssem,
    m_rsem,
    x_ssem,
    x_rsem,
    ap_ssem,
    ap_rsem,
    am_ssem,
    am_rsem,
    c_ssem,
    c_rsem,
    u_ssem,
    u_rsem,
    d_ssem,
    d_rsem,
    out_sem,
):
    ny = n_vec // 4
    plus, minus = ny // 2, ny // 2 - 1
    rows = PACK // ny
    wide = w.shape[2]
    row, vec = lax.axis_index("row"), lax.axis_index("vec")
    y, half, core = vec // 4, (vec // 2) % 2, vec % 2
    up = (row, ((y + 1) % ny) * 4 + vec % 4)
    down = (row, ((y + ny - 1) % ny) * 4 + vec % 4)
    sib = (row, vec + 1 - 2 * core)
    across = (row, vec + 2 - 4 * half)
    below = ((row + 1) % n_row, vec)
    above = ((row + n_row - 1) % n_row, vec)
    other = 1 - core

    def remote(src, dst, ssem, rsem, to):
        return pltpu.make_async_remote_copy(
            src_ref=src, dst_ref=dst, send_sem=ssem, recv_sem=rsem, device_id=to, device_id_type=MESH
        )

    stage = [
        pltpu.make_async_copy(v_hbm.at[0, 0, :, pl.ds(0, H)], blk.at[0, pl.ds(0, 512)], in_sem.at[0]),
        pltpu.make_async_copy(v_hbm.at[0, 0, :, pl.ds(H, H)], blk.at[1, pl.ds(0, 512)], in_sem.at[1]),
        pltpu.make_async_copy(s_hbm.at[0, 0, pl.ds(0, 128), pl.ds(0, H)], blk.at[0, pl.ds(512, 128)], in_sem.at[2]),
        pltpu.make_async_copy(s_hbm.at[0, 0, pl.ds(192, 64), pl.ds(H, H)], blk.at[0, pl.ds(640, 64)], in_sem.at[3]),
        pltpu.make_async_copy(s_hbm.at[0, 0, pl.ds(0, 192), pl.ds(H, H)], blk.at[1, pl.ds(512, 192)], in_sem.at[4]),
    ]
    firsts = [
        pltpu.make_async_copy(slab.at[pl.ds(0, R), pl.ds(c * wide, wide)], first.at[c], in_sem.at[5 + c])
        for c in range(NC)
    ]
    loads = [
        pltpu.make_async_copy(slab.at[:, pl.ds(c * wide, wide)], w.at[c], in_sem.at[5 + NC + c]) for c in range(NC)
    ]
    for copy in stage + firsts + loads:
        copy.start()

    barrier = pltpu.get_barrier_semaphore()
    for to in (up, down, sib, across, below, above):
        pl.semaphore_signal(barrier, inc=1, device_id=to, device_id_type=MESH)
    pl.semaphore_wait(barrier, 6)

    for copy in stage:
        copy.wait()
    raw = remote(blk.at[other], sib_blk, raw_sem.at[0], raw_sem.at[1], sib)
    raw.start()

    def d_copy(k, src):
        return remote(src, din.at[k], d_ssem.at[k], d_rsem.at[k], above)

    for c in range(NC):
        firsts[c].wait()
        d_copy(c, first.at[c]).start()

    roots = [index[f, row] for f in range(FRONTS)]
    chip = [lax.shift_right_logical(root, 1) for root in roots]
    side = [lax.bitwise_and(part, 1) for part in chip]
    line = [lax.shift_right_logical(root, 2) for root in roots]

    def piece(o):
        return pl.ds(pl.multiple_of(o * rows, 8), rows)

    def candidate(f, o):
        return where(roots[f], sib[1], sib_blk[piece(o), :], blk[core, piece(o), :])

    def p_copy(f, s):
        i = f * plus + s
        return remote(ps.at[i], pr.at[i], p_ssem.at[i], p_rsem.at[i], up)

    def m_copy(f, s):
        i = f * minus + s
        return remote(ms.at[i], mr.at[i], m_ssem.at[i], m_rsem.at[i], down)

    def x_copy(f):
        return remote(xs.at[f], xr.at[f], x_ssem.at[f], x_rsem.at[f], across)

    def ap_copy(f, s):
        at = vb.at[f, core, piece((y + ny - s) % ny)]
        return remote(at, at, ap_ssem.at[f * plus + s], ap_rsem.at[f * plus + s], up)

    def ap_wait(f, s):
        at = vb.at[f, core, piece((y + ny - 1 - s) % ny)]
        remote(at, at, ap_ssem.at[f * plus + s], ap_rsem.at[f * plus + s], up).wait_recv()

    def am_copy(f, s):
        at = vb.at[f, core, piece((y + s) % ny)]
        return remote(at, at, am_ssem.at[f * minus + s], am_rsem.at[f * minus + s], down)

    def am_wait(f, s):
        at = vb.at[f, core, piece((y + 1 + s) % ny)]
        remote(at, at, am_ssem.at[f * minus + s], am_rsem.at[f * minus + s], down).wait_recv()

    def c_copy(f, t, o):
        at = vb.at[f, core, piece(o)]
        return remote(at, at, c_ssem.at[f * ny + t], c_rsem.at[f * ny + t], sib)

    def c_wait(f, t, o):
        at = vb.at[f, other, piece(o)]
        remote(at, at, c_ssem.at[f * ny + t], c_rsem.at[f * ny + t], sib).wait_recv()

    def slots():
        yield 0, y
        for s in range(plus):
            yield 1 + s, (y + ny - 1 - s) % ny
        for s in range(minus):
            yield 1 + plus + s, (y + 1 + s) % ny

    raw.wait_recv()
    for s in range(plus):
        for f in range(FRONTS):
            mine = candidate(f, (y + plus - s) % ny)
            if s > 0:
                p_copy(f, s - 1).wait_recv()
                mine = where(chip[f], vec // 2, mine, pr[f * plus + s - 1])
            ps[f * plus + s] = mine
            if s < minus:
                back = candidate(f, (y + ny - minus + s) % ny)
                if s > 0:
                    m_copy(f, s - 1).wait_recv()
                    back = where(chip[f], vec // 2, back, mr[f * minus + s - 1])
                ms[f * minus + s] = back
            p_copy(f, s).start()
            if s < minus:
                m_copy(f, s).start()
    for f in range(FRONTS):
        p_copy(f, plus - 1).wait_recv()
        m_copy(f, minus - 1).wait_recv()
        got = pr[f * plus + plus - 1]
        for s in range(minus):
            got = where(line[f], (y + 1 + s) % ny, mr[f * minus + minus - 1], got)
        xs[f] = where(chip[f], vec // 2, candidate(f, y), got)
        x_copy(f).start()
    for f in range(FRONTS):
        x_copy(f).wait_recv()
        vb[f, core, piece(y), :] = where(side[f], half, xs[f], xr[f])
        ap_copy(f, 0).start()
        am_copy(f, 0).start()
        c_copy(f, 0, y).start()
    for s in range(plus):
        for f in range(FRONTS):
            ap_wait(f, s)
            if s + 1 < plus:
                ap_copy(f, s + 1).start()
            c_copy(f, 1 + s, (y + ny - 1 - s) % ny).start()
            if s < minus:
                am_wait(f, s)
                if s + 1 < minus:
                    am_copy(f, s + 1).start()
                c_copy(f, 1 + plus + s, (y + 1 + s) % ny).start()
    for f in range(FRONTS):
        for t, o in slots():
            c_wait(f, t, o)

    def prepare(f):
        place = offset[f, row]
        for j in range(2):
            block = vb[f, j, 0:512, :]
            v_h[f, :, j * H : (j + 1) * H], v_l[f, :, j * H : (j + 1) * H] = split(block)
            vt_h[f, j * H : (j + 1) * H, :], vt_l[f, j * H : (j + 1) * H, :] = split(block.T)
        upper = lax.broadcasted_iota(jnp.int32, (H, H), 0) <= lax.broadcasted_iota(jnp.int32, (H, H), 1)
        a = jnp.where(upper, vb[f, 0, 512:640, :], 0.0)
        b = vb[f, 1, 512:640, :]
        c = jnp.where(upper, jnp.concatenate([vb[f, 1, 640:704, :], vb[f, 0, 640:704, :]], axis=0), 0.0)
        zero = jnp.zeros((H, H), F32)
        crossing = 3 + row // (n_row - 1)
        for i, j, part in ((0, 0, a), (0, 1, b), (1, 0, zero), (1, 1, c)):
            at = (f, slice(i * H, (i + 1) * H), slice(j * H, (j + 1) * H))
            high, low = split(where(place, crossing, part, zero))
            sx_h[at], sx_l[at] = high, low
            high, low = split(where(place, crossing, zero, part))
            so_h[at], so_l[at] = high, low

    for copy in loads:
        copy.wait()
    prepare(0)

    def u_copy(k):
        return remote(uout.at[k], uin.at[k], u_ssem.at[k], u_rsem.at[k], below)

    def cross(k):
        f, c = k // NC, k % NC
        d_copy(k, dout.at[0]).wait_recv()
        bottom, top = w[c, 3 * R : 4 * R, :], din[k]
        b, t = split(bottom), split(top)
        inner = mm((vt_h[f, :, 0:R], vt_l[f, :, 0:R]), b) + mm((vt_h[f, :, R : 2 * R], vt_l[f, :, R : 2 * R]), t)
        mixed = split(mm((sx_h[f], sx_l[f]), split(inner)))
        uout[k] = top - mm((v_h[f, R : 2 * R, :], v_l[f, R : 2 * R, :]), mixed)
        w[c, 3 * R : 4 * R, :] = bottom - mm((v_h[f, 0:R, :], v_l[f, 0:R, :]), mixed)
        u_copy(k).start()

    def out_copy(c):
        return pltpu.make_async_copy(w.at[c], out.at[:, pl.ds(c * wide, wide)], out_sem.at[c])

    def own(k):
        f, c = k // NC, k % NC
        place = offset[f, row]
        u_copy(k).wait_recv()
        parts = [uin[k]] + [w[c, b * R : (b + 1) * R, :] for b in range(1, 4)]
        window = [where(place, 0, parts[i], where(place, 1, parts[1 + i], parts[2 + i])) for i in range(2)]
        window = split(jnp.concatenate(window, axis=0))
        inner = mm((vt_h[f], vt_l[f]), window)
        mixed = split(mm((so_h[f], so_l[f]), split(inner)))
        pad[...] = mm((v_h[f], v_l[f]), mixed)
        none = jnp.zeros((R, wide), F32)

        def fresh(b):
            old = uin[k] if b == 0 else w[c, b * R : (b + 1) * R, :]
            lower = where(place, b - 1, pad[R : 2 * R, :], none) if b > 0 else none
            return old - where(place, b, pad[0:R, :], lower)

        top = fresh(0)
        w[c, 0:R, :] = top

        @pl.when(k < (FRONTS - 1) * NC)
        def _():
            dout[k] = top

        for b in range(1, 4):
            w[c, b * R : (b + 1) * R, :] = fresh(b)

        @pl.when(k < (FRONTS - 1) * NC)
        def _():
            d_copy(k + NC, dout.at[k]).start()

        @pl.when(k >= (FRONTS - 1) * NC)
        def _():
            pltpu.make_async_copy(
                w.at[c], out.at[:, pl.ds(pl.multiple_of(c * wide, wide), wide)], out_sem.at[c]
            ).start()

    def step(k, carry):
        @pl.when(k < FRONTS * NC)
        def _():
            cross(k)

        @pl.when(jnp.logical_or(k == 2, k == 3))
        def _():
            prepare(k - 1)

        @pl.when(k >= 2)
        def _():
            own(k - 2)

        return carry

    lax.fori_loop(0, FRONTS * NC + 2, step, 0)

    raw.wait_send()
    for f in range(FRONTS):
        x_copy(f).wait_send()
        for s in range(plus):
            p_copy(f, s).wait_send()
            ap_copy(f, s).wait_send()
        for s in range(minus):
            m_copy(f, s).wait_send()
            am_copy(f, s).wait_send()
        for t, o in slots():
            c_copy(f, t, o).wait_send()
    for k in range(FRONTS * NC):
        u_copy(k).wait_send()
        d_copy(k, dout.at[0]).wait_send()
    for c in range(NC):
        out_copy(c).wait()


def solution(mesh):
    n_row, n_vec = mesh.shape["row"], mesh.shape["vec"]
    ny = n_vec // 4
    plus, minus = ny // 2, ny // 2 - 1

    def body(vectors, block_index, block_offset, reflector_vectors, reflector_factors):
        wide = vectors.shape[1] // NC
        steps = FRONTS * NC
        dma = pltpu.SemaphoreType.DMA
        hbm, smem = pl.BlockSpec(memory_space=pl.ANY), pl.BlockSpec(memory_space=pltpu.SMEM)
        vmem = pltpu.VMEM
        rows = PACK // ny
        return pl.pallas_call(
            functools.partial(kernel, n_row, n_vec),
            out_shape=jax.ShapeDtypeStruct(vectors.shape, F32),
            in_specs=[hbm, smem, smem, hbm, hbm],
            out_specs=hbm,
            scratch_shapes=[
                vmem((NC, 4 * R, wide), F32),
                vmem((NC, R, wide), F32),
                vmem((steps, R, wide), F32),
                vmem((steps, R, wide), F32),
                vmem((steps, R, wide), F32),
                vmem((steps - NC, R, wide), F32),
                vmem((2 * R, wide), F32),
                vmem((2, PACK, H), F32),
                vmem((PACK, H), F32),
                vmem((FRONTS, 2, PACK, H), F32),
                vmem((FRONTS * plus, rows, H), F32),
                vmem((FRONTS * plus, rows, H), F32),
                vmem((FRONTS * minus, rows, H), F32),
                vmem((FRONTS * minus, rows, H), F32),
                vmem((FRONTS, rows, H), F32),
                vmem((FRONTS, rows, H), F32),
                vmem((FRONTS, R, 2 * R), BF16),
                vmem((FRONTS, R, 2 * R), BF16),
                vmem((FRONTS, 2 * R, R), BF16),
                vmem((FRONTS, 2 * R, R), BF16),
                vmem((FRONTS, R, R), BF16),
                vmem((FRONTS, R, R), BF16),
                vmem((FRONTS, R, R), BF16),
                vmem((FRONTS, R, R), BF16),
                dma((5 + 2 * NC,)),
                dma((2,)),
                dma((FRONTS * plus,)),
                dma((FRONTS * plus,)),
                dma((FRONTS * minus,)),
                dma((FRONTS * minus,)),
                dma((FRONTS,)),
                dma((FRONTS,)),
                dma((FRONTS * plus,)),
                dma((FRONTS * plus,)),
                dma((FRONTS * minus,)),
                dma((FRONTS * minus,)),
                dma((FRONTS * ny,)),
                dma((FRONTS * ny,)),
                dma((steps,)),
                dma((steps,)),
                dma((steps,)),
                dma((steps,)),
                dma((NC,)),
            ],
            compiler_params=pltpu.CompilerParams(
                collective_id=0, has_side_effects=True, vmem_limit_bytes=48 * 1024 * 1024
            ),
            name="fronts",
        )(vectors, block_index, block_offset, reflector_vectors, reflector_factors)

    return jax.shard_map(
        body,
        mesh=mesh,
        in_specs=(P("row", "vec"), P(), P(), P("row", "vec", None, None), P("row", "vec", None, None)),
        out_specs=P("row", "vec"),
        check_vma=False,
    )
```

```python
import functools

import jax
import jax.numpy as jnp
from jax import lax
from jax.experimental import pallas as pl
from jax.experimental.pallas import tpu as pltpu
from jax.sharding import PartitionSpec as P

MESH = pl.DeviceIdType.MESH
F32, BF16 = jnp.float32, jnp.bfloat16
FRONTS = 3
PREV = FRONTS
R = 256
H = 128
PACK = 704
NC = 4


def split(x):
    high = x.astype(BF16)
    return high, (x - high.astype(F32)).astype(BF16)


def where(value, target, yes, no):
    return jnp.where(jnp.full(yes.shape, value, jnp.int32) == jnp.full(yes.shape, target, jnp.int32), yes, no)


def mm(a, b):
    dot = functools.partial(jnp.dot, preferred_element_type=F32)
    return dot(a[0], b[0]) + (dot(a[0], b[1]) + dot(a[1], b[0]))


def kernel(
    n_row,
    n_vec,
    slab,
    index_hbm,
    offset_hbm,
    v_hbm,
    s_hbm,
    out,
    index,
    offset,
    w,
    first,
    last,
    bin_,
    din,
    dout,
    bout,
    pad,
    blk,
    sib_blk,
    vb,
    ps,
    pr,
    ms,
    mr,
    xs,
    xr,
    vt_h,
    vt_l,
    v_h,
    v_l,
    s_h,
    s_l,
    in_sem,
    raw_sem,
    p_ssem,
    p_rsem,
    m_ssem,
    m_rsem,
    x_ssem,
    x_rsem,
    z_ssem,
    z_rsem,
    ap_ssem,
    ap_rsem,
    am_ssem,
    am_rsem,
    c_ssem,
    c_rsem,
    d_ssem,
    d_rsem,
    b_ssem,
    b_rsem,
    out_sem,
):
    ny = n_vec // 4
    plus, minus = ny // 2, ny // 2 - 1
    rows = PACK // ny
    wide = w.shape[2]
    row, vec = lax.axis_index("row"), lax.axis_index("vec")
    y, half, core = vec // 4, (vec // 2) % 2, vec % 2
    up = (row, ((y + 1) % ny) * 4 + vec % 4)
    down = (row, ((y + ny - 1) % ny) * 4 + vec % 4)
    sib = (row, vec + 1 - 2 * core)
    across = (row, vec + 2 - 4 * half)
    below = ((row + 1) % n_row, vec)
    above = ((row + n_row - 1) % n_row, vec)
    other = 1 - core

    def remote(src, dst, ssem, rsem, to):
        return pltpu.make_async_remote_copy(
            src_ref=src, dst_ref=dst, send_sem=ssem, recv_sem=rsem, device_id=to, device_id_type=MESH
        )

    stage = [
        pltpu.make_async_copy(v_hbm.at[0, 0, :, pl.ds(0, H)], blk.at[0, pl.ds(0, 512)], in_sem.at[0]),
        pltpu.make_async_copy(v_hbm.at[0, 0, :, pl.ds(H, H)], blk.at[1, pl.ds(0, 512)], in_sem.at[1]),
        pltpu.make_async_copy(s_hbm.at[0, 0, pl.ds(0, 128), pl.ds(0, H)], blk.at[0, pl.ds(512, 128)], in_sem.at[2]),
        pltpu.make_async_copy(s_hbm.at[0, 0, pl.ds(192, 64), pl.ds(H, H)], blk.at[0, pl.ds(640, 64)], in_sem.at[3]),
        pltpu.make_async_copy(s_hbm.at[0, 0, pl.ds(0, 192), pl.ds(H, H)], blk.at[1, pl.ds(512, 192)], in_sem.at[4]),
        pltpu.make_async_copy(index_hbm, index, in_sem.at[5 + 3 * NC]),
        pltpu.make_async_copy(offset_hbm, offset, in_sem.at[6 + 3 * NC]),
    ]
    firsts = [
        pltpu.make_async_copy(slab.at[pl.ds(0, R), pl.ds(c * wide, wide)], first.at[c], in_sem.at[5 + c])
        for c in range(NC)
    ]
    lasts = [
        pltpu.make_async_copy(slab.at[pl.ds(3 * R, R), pl.ds(c * wide, wide)], last.at[c], in_sem.at[5 + NC + c])
        for c in range(NC)
    ]
    loads = [
        pltpu.make_async_copy(slab.at[:, pl.ds(c * wide, wide)], w.at[c], in_sem.at[5 + 2 * NC + c])
        for c in range(NC)
    ]
    for copy in stage + firsts + lasts + loads:
        copy.start()

    barrier = pltpu.get_barrier_semaphore()
    for to in (up, down, sib, across, below, above):
        pl.semaphore_signal(barrier, inc=1, device_id=to, device_id_type=MESH)
    pl.semaphore_wait(barrier, 6)

    for copy in stage:
        copy.wait()
    raw = remote(blk.at[other], sib_blk, raw_sem.at[0], raw_sem.at[1], sib)
    raw.start()

    def d_copy(k, src):
        return remote(src, din.at[k], d_ssem.at[k], d_rsem.at[k], above)

    def b_copy(k, src):
        return remote(src, bin_.at[k], b_ssem.at[k], b_rsem.at[k], below)

    for c in range(NC):
        firsts[c].wait()
        d_copy(c, first.at[c]).start()
        lasts[c].wait()
        b_copy(c, last.at[c]).start()

    roots = [index[f, row] for f in range(FRONTS)]
    chip = [lax.shift_right_logical(root, 1) for root in roots]
    side = [lax.bitwise_and(part, 1) for part in chip]
    line = [lax.shift_right_logical(root, 2) for root in roots]

    def piece(o):
        return pl.ds(pl.multiple_of(o * rows, 8), rows)

    def candidate(f, o):
        return where(roots[f], sib[1], sib_blk[piece(o), :], blk[core, piece(o), :])

    def p_copy(f, s):
        i = f * plus + s
        return remote(ps.at[i], pr.at[i], p_ssem.at[i], p_rsem.at[i], up)

    def m_copy(f, s):
        i = f * minus + s
        return remote(ms.at[i], mr.at[i], m_ssem.at[i], m_rsem.at[i], down)

    def x_copy(f):
        return remote(xs.at[f], xr.at[f], x_ssem.at[f], x_rsem.at[f], across)

    def ap_copy(f, s):
        at = vb.at[f, core, piece((y + ny - s) % ny)]
        return remote(at, at, ap_ssem.at[f * plus + s], ap_rsem.at[f * plus + s], up)

    def ap_wait(f, s):
        at = vb.at[f, core, piece((y + ny - 1 - s) % ny)]
        remote(at, at, ap_ssem.at[f * plus + s], ap_rsem.at[f * plus + s], up).wait_recv()

    def am_copy(f, s):
        at = vb.at[f, core, piece((y + s) % ny)]
        return remote(at, at, am_ssem.at[f * minus + s], am_rsem.at[f * minus + s], down)

    def am_wait(f, s):
        at = vb.at[f, core, piece((y + 1 + s) % ny)]
        remote(at, at, am_ssem.at[f * minus + s], am_rsem.at[f * minus + s], down).wait_recv()

    def c_copy(f, t, o):
        at = vb.at[f, core, piece(o)]
        return remote(at, at, c_ssem.at[f * ny + t], c_rsem.at[f * ny + t], sib)

    def c_wait(f, t, o):
        at = vb.at[f, other, piece(o)]
        remote(at, at, c_ssem.at[f * ny + t], c_rsem.at[f * ny + t], sib).wait_recv()

    def slots():
        yield 0, y
        for s in range(plus):
            yield 1 + s, (y + ny - 1 - s) % ny
        for s in range(minus):
            yield 1 + plus + s, (y + 1 + s) % ny

    def z_copy(f):
        src, dst = vb.at[f, core, piece(y)], vb.at[PREV + f, core, piece(y)]
        return remote(src, dst, z_ssem.at[f], z_rsem.at[f], below)

    def select(f, s):
        mine = candidate(f, (y + plus - s) % ny)
        if s > 0:
            p_copy(f, s - 1).wait_recv()
            mine = where(chip[f], vec // 2, mine, pr[f * plus + s - 1])
        ps[f * plus + s] = mine
        if s < minus:
            back = candidate(f, (y + ny - minus + s) % ny)
            if s > 0:
                m_copy(f, s - 1).wait_recv()
                back = where(chip[f], vec // 2, back, mr[f * minus + s - 1])
            ms[f * minus + s] = back
        p_copy(f, s).start()
        if s < minus:
            m_copy(f, s).start()

    def swap(f):
        p_copy(f, plus - 1).wait_recv()
        m_copy(f, minus - 1).wait_recv()
        got = pr[f * plus + plus - 1]
        for s in range(minus):
            got = where(line[f], (y + 1 + s) % ny, mr[f * minus + minus - 1], got)
        xs[f] = where(chip[f], vec // 2, candidate(f, y), got)
        x_copy(f).start()

    def begin(g):
        if g >= PREV:
            z_copy(g - PREV).wait_recv()
        else:
            x_copy(g).wait_recv()
            vb[g, core, piece(y), :] = where(side[g], half, xs[g], xr[g])
        ap_copy(g, 0).start()
        am_copy(g, 0).start()
        if g < PREV:
            z_copy(g).start()
        c_copy(g, 0, y).start()

    def gather(g, s):
        ap_wait(g, s)
        if s + 1 < plus:
            ap_copy(g, s + 1).start()
        if s < minus:
            am_wait(g, s)
            if s + 1 < minus:
                am_copy(g, s + 1).start()
        c_copy(g, 1 + s, (y + ny - 1 - s) % ny).start()
        if s < minus:
            c_copy(g, 1 + plus + s, (y + 1 + s) % ny).start()

    def whole(g):
        for t, o in slots():
            c_wait(g, t, o)

    delay = {0: 0, PREV: 1, 1: 1, PREV + 1: 2, 2: 3, PREV + 2: 4}

    def tick(t):
        for g, late in delay.items():
            s = t - late - 1
            if s == -1:
                begin(g)
            elif 0 <= s < plus:
                gather(g, s)

    raw.wait_recv()
    for s in range(plus):
        for f in range(FRONTS):
            select(f, s)
    for f in range(FRONTS):
        swap(f)

    def prepare(f):
        for j in range(2):
            block = vb[f, j, 0:512, :]
            v_h[f, :, j * H : (j + 1) * H], v_l[f, :, j * H : (j + 1) * H] = split(block)
            vt_h[f, j * H : (j + 1) * H, :], vt_l[f, j * H : (j + 1) * H, :] = split(block.T)
        upper = lax.broadcasted_iota(jnp.int32, (H, H), 0) <= lax.broadcasted_iota(jnp.int32, (H, H), 1)
        a = jnp.where(upper, vb[f, 0, 512:640, :], 0.0)
        b = vb[f, 1, 512:640, :]
        c = jnp.where(upper, jnp.concatenate([vb[f, 1, 640:704, :], vb[f, 0, 640:704, :]], axis=0), 0.0)
        zero = jnp.zeros((H, H), F32)
        if f >= PREV:
            place, crossing = offset[f - PREV, above[0]], 3 + (n_row - row) // n_row
        for i, j, part in ((0, 0, a), (0, 1, b), (1, 0, zero), (1, 1, c)):
            at = (f, slice(i * H, (i + 1) * H), slice(j * H, (j + 1) * H))
            s_h[at], s_l[at] = split(where(place, crossing, part, zero) if f >= PREV else part)

    for t in range(plus + 1):
        tick(t)
    for copy in loads:
        copy.wait()
    whole(0)
    prepare(0)
    tick(plus + 1)
    whole(PREV)
    prepare(PREV)

    def out_copy(c):
        return pltpu.make_async_copy(w.at[c], out.at[:, pl.ds(c * wide, wide)], out_sem.at[c])

    def edge(f, c, k):
        g = PREV + f
        b, t = split(bin_[k]), split(w[c, 0:R, :])
        inner = mm((vt_h[g, :, 0:R], vt_l[g, :, 0:R]), b) + mm((vt_h[g, :, R : 2 * R], vt_l[g, :, R : 2 * R]), t)
        mixed = split(mm((s_h[g], s_l[g]), split(inner)))
        w[c, 0:R, :] = w[c, 0:R, :] - mm((v_h[g, R : 2 * R, :], v_l[g, R : 2 * R, :]), mixed)

    def own(f, c, k):
        place = offset[f, row]
        parts = [w[c, b * R : (b + 1) * R, :] for b in range(4)] + [din[k]]
        window = [parts[3 + i] for i in range(2)]
        for b in (2, 1, 0):
            window = [where(place, b, parts[b + i], window[i]) for i in range(2)]
        inner = mm((vt_h[f], vt_l[f]), split(jnp.concatenate(window, axis=0)))
        mixed = split(mm((s_h[f], s_l[f]), split(inner)))
        pad[...] = mm((v_h[f], v_l[f]), mixed)
        none = jnp.zeros((R, wide), F32)

        def fresh(b):
            lower = where(place, b - 1, pad[R : 2 * R, :], none) if b > 0 else none
            return w[c, b * R : (b + 1) * R, :] - where(place, b, pad[0:R, :], lower)

        top, bottom = fresh(0), fresh(3)

        @pl.when(k < (FRONTS - 1) * NC)
        def _():
            dout[k] = top
            bout[k] = bottom

        w[c, 0:R, :] = top
        w[c, 3 * R : 4 * R, :] = bottom
        for b in (1, 2):
            w[c, b * R : (b + 1) * R, :] = fresh(b)

        @pl.when(k < (FRONTS - 1) * NC)
        def _():
            d_copy(k + NC, dout.at[k]).start()
            b_copy(k + NC, bout.at[k]).start()

        @pl.when(k >= (FRONTS - 1) * NC)
        def _():
            pltpu.make_async_copy(
                w.at[c], out.at[:, pl.ds(pl.multiple_of(c * wide, wide), wide)], out_sem.at[c]
            ).start()

    def step(k, carry):
        @pl.when(k == 2)
        def _():
            tick(plus + 2)

        @pl.when(k == 4)
        def _():
            tick(plus + 3)
            for g in (1, PREV + 1):
                whole(g)
                prepare(g)

        @pl.when(k == 6)
        def _():
            tick(plus + 4)

        @pl.when(k == 8)
        def _():
            for g in (2, PREV + 2):
                whole(g)
                prepare(g)

        d_copy(k, dout.at[0]).wait_recv()
        b_copy(k, bout.at[0]).wait_recv()
        f, c = k // NC, k % NC
        edge(f, c, k)
        own(f, c, k)
        return carry

    lax.fori_loop(0, FRONTS * NC, step, 0)

    raw.wait_send()
    for f in range(2 * FRONTS):
        if f < FRONTS:
            x_copy(f).wait_send()
            z_copy(f).wait_send()
            for s in range(plus):
                p_copy(f, s).wait_send()
            for s in range(minus):
                m_copy(f, s).wait_send()
        for s in range(plus):
            ap_copy(f, s).wait_send()
        for s in range(minus):
            am_copy(f, s).wait_send()
        for t, o in slots():
            c_copy(f, t, o).wait_send()
    for k in range(FRONTS * NC):
        d_copy(k, dout.at[0]).wait_send()
        b_copy(k, bout.at[0]).wait_send()
    for c in range(NC):
        out_copy(c).wait()


def solution(mesh):
    n_row, n_vec = mesh.shape["row"], mesh.shape["vec"]
    ny = n_vec // 4
    plus, minus = ny // 2, ny // 2 - 1

    def body(vectors, block_index, block_offset, reflector_vectors, reflector_factors):
        wide = vectors.shape[1] // NC
        steps = FRONTS * NC
        dma = pltpu.SemaphoreType.DMA
        hbm = pl.BlockSpec(memory_space=pltpu.HBM)
        vmem = pltpu.VMEM
        rows = PACK // ny
        return pl.pallas_call(
            functools.partial(kernel, n_row, n_vec),
            out_shape=jax.ShapeDtypeStruct(vectors.shape, F32),
            in_specs=[hbm] * 5,
            out_specs=pl.BlockSpec(memory_space=pl.ANY),
            scratch_shapes=[
                pltpu.SMEM((FRONTS, n_row), jnp.int32),
                pltpu.SMEM((FRONTS, n_row), jnp.int32),
                vmem((NC, 4 * R, wide), F32),
                vmem((NC, R, wide), F32),
                vmem((NC, R, wide), F32),
                vmem((steps, R, wide), F32),
                vmem((steps, R, wide), F32),
                vmem((steps - NC, R, wide), F32),
                vmem((steps - NC, R, wide), F32),
                vmem((2 * R, wide), F32),
                vmem((2, PACK, H), F32),
                vmem((PACK, H), F32),
                vmem((2 * FRONTS, 2, PACK, H), F32),
                vmem((FRONTS * plus, rows, H), F32),
                vmem((FRONTS * plus, rows, H), F32),
                vmem((FRONTS * minus, rows, H), F32),
                vmem((FRONTS * minus, rows, H), F32),
                vmem((FRONTS, rows, H), F32),
                vmem((FRONTS, rows, H), F32),
                vmem((2 * FRONTS, R, 2 * R), BF16),
                vmem((2 * FRONTS, R, 2 * R), BF16),
                vmem((2 * FRONTS, 2 * R, R), BF16),
                vmem((2 * FRONTS, 2 * R, R), BF16),
                vmem((2 * FRONTS, R, R), BF16),
                vmem((2 * FRONTS, R, R), BF16),
                dma((7 + 3 * NC,)),
                dma((2,)),
                dma((FRONTS * plus,)),
                dma((FRONTS * plus,)),
                dma((FRONTS * minus,)),
                dma((FRONTS * minus,)),
                dma((FRONTS,)),
                dma((FRONTS,)),
                dma((FRONTS,)),
                dma((FRONTS,)),
                dma((2 * FRONTS * plus,)),
                dma((2 * FRONTS * plus,)),
                dma((2 * FRONTS * minus,)),
                dma((2 * FRONTS * minus,)),
                dma((2 * FRONTS * ny,)),
                dma((2 * FRONTS * ny,)),
                dma((steps,)),
                dma((steps,)),
                dma((steps,)),
                dma((steps,)),
                dma((NC,)),
            ],
            compiler_params=pltpu.CompilerParams(
                collective_id=0, has_side_effects=True, vmem_limit_bytes=48 * 1024 * 1024
            ),
            name="fronts",
        )(
            *(
                pltpu.with_memory_space_constraint(array, pltpu.HBM)
                for array in (vectors, block_index, block_offset, reflector_vectors, reflector_factors)
            )
        )

    return jax.shard_map(
        body,
        mesh=mesh,
        in_specs=(P("row", "vec"), P(), P(), P("row", "vec", None, None), P("row", "vec", None, None)),
        out_specs=P("row", "vec"),
        check_vma=False,
    )
```

```python
import functools

import jax
import jax.numpy as jnp
from jax import lax
from jax.experimental import pallas as pl
from jax.experimental.pallas import tpu as pltpu
from jax.sharding import PartitionSpec as P

MESH = pl.DeviceIdType.MESH
F32, BF16 = jnp.float32, jnp.bfloat16
FRONTS = 3
PREV = FRONTS
R = 256
H = 128
PACK = 704
NC = 4


def streams(rows):
    cut = (rows // 8 + 1) // 2 * 8
    return ((0, 0, cut), (0, cut, rows - cut), (1, 0, rows), (2, 0, rows))


def split(x):
    high = x.astype(BF16)
    return high, (x - high.astype(F32)).astype(BF16)


def where(value, target, yes, no):
    return jnp.where(jnp.full(yes.shape, value, jnp.int32) == jnp.full(yes.shape, target, jnp.int32), yes, no)


def mm(a, b):
    dot = functools.partial(jnp.dot, preferred_element_type=F32)
    return dot(a[0], b[0]) + (dot(a[0], b[1]) + dot(a[1], b[0]))


def kernel(
    n_row,
    n_vec,
    slab,
    index_hbm,
    offset_hbm,
    v_hbm,
    s_hbm,
    out,
    index,
    offset,
    w,
    first,
    last,
    bin_,
    din,
    dout,
    bout,
    pad,
    blk,
    sib_blk,
    vb,
    ps,
    pr,
    ms,
    mr,
    xs,
    xr,
    same_r,
    cross_r,
    vt_h,
    vt_l,
    v_h,
    v_l,
    s_h,
    s_l,
    in_sem,
    raw_sem,
    p_ssem,
    p_rsem,
    m_ssem,
    m_rsem,
    x_ssem,
    x_rsem,
    z_ssem,
    z_rsem,
    same_ssem,
    same_rsem,
    cross_ssem,
    cross_rsem,
    ap_ssem,
    ap_rsem,
    am_ssem,
    am_rsem,
    c_ssem,
    c_rsem,
    d_ssem,
    d_rsem,
    b_ssem,
    b_rsem,
    out_sem,
):
    ny = n_vec // 4
    plus, minus = ny // 2, ny // 2 - 1
    rows = PACK // ny
    wide = w.shape[2]
    row, vec = lax.axis_index("row"), lax.axis_index("vec")
    y, half, core = vec // 4, (vec // 2) % 2, vec % 2
    up = (row, ((y + 1) % ny) * 4 + vec % 4)
    down = (row, ((y + ny - 1) % ny) * 4 + vec % 4)
    sib = (row, vec + 1 - 2 * core)
    across = (row, vec + 2 - 4 * half)
    below = ((row + 1) % n_row, vec)
    across_below = (below[0], across[1])
    above = ((row + n_row - 1) % n_row, vec)
    across_above = (above[0], across[1])
    other = 1 - core

    def remote(src, dst, ssem, rsem, to):
        return pltpu.make_async_remote_copy(
            src_ref=src, dst_ref=dst, send_sem=ssem, recv_sem=rsem, device_id=to, device_id_type=MESH
        )

    stage = [
        pltpu.make_async_copy(v_hbm.at[0, 0, :, pl.ds(0, H)], blk.at[0, pl.ds(0, 512)], in_sem.at[0]),
        pltpu.make_async_copy(v_hbm.at[0, 0, :, pl.ds(H, H)], blk.at[1, pl.ds(0, 512)], in_sem.at[1]),
        pltpu.make_async_copy(s_hbm.at[0, 0, pl.ds(0, 128), pl.ds(0, H)], blk.at[0, pl.ds(512, 128)], in_sem.at[2]),
        pltpu.make_async_copy(s_hbm.at[0, 0, pl.ds(192, 64), pl.ds(H, H)], blk.at[0, pl.ds(640, 64)], in_sem.at[3]),
        pltpu.make_async_copy(s_hbm.at[0, 0, pl.ds(0, 192), pl.ds(H, H)], blk.at[1, pl.ds(512, 192)], in_sem.at[4]),
        pltpu.make_async_copy(index_hbm, index, in_sem.at[5 + 3 * NC]),
        pltpu.make_async_copy(offset_hbm, offset, in_sem.at[6 + 3 * NC]),
    ]
    firsts = [
        pltpu.make_async_copy(slab.at[pl.ds(0, R), pl.ds(c * wide, wide)], first.at[c], in_sem.at[5 + c])
        for c in range(NC)
    ]
    lasts = [
        pltpu.make_async_copy(slab.at[pl.ds(3 * R, R), pl.ds(c * wide, wide)], last.at[c], in_sem.at[5 + NC + c])
        for c in range(NC)
    ]
    loads = [
        pltpu.make_async_copy(slab.at[:, pl.ds(c * wide, wide)], w.at[c], in_sem.at[5 + 2 * NC + c])
        for c in range(NC)
    ]
    for copy in stage + firsts + lasts + loads:
        copy.start()

    barrier = pltpu.get_barrier_semaphore()
    for to in (up, down, sib, across, below, above, across_below, across_above):
        pl.semaphore_signal(barrier, inc=1, device_id=to, device_id_type=MESH)
    pl.semaphore_wait(barrier, 8)

    for copy in stage:
        copy.wait()
    raw = remote(blk.at[other], sib_blk, raw_sem.at[0], raw_sem.at[1], sib)
    raw.start()

    def d_copy(k, src):
        return remote(src, din.at[k], d_ssem.at[k], d_rsem.at[k], above)

    def b_copy(k, src):
        return remote(src, bin_.at[k], b_ssem.at[k], b_rsem.at[k], below)

    for c in range(NC):
        firsts[c].wait()
        d_copy(c, first.at[c]).start()
        lasts[c].wait()
        b_copy(c, last.at[c]).start()

    roots = [index[f, row] for f in range(FRONTS)]
    chip = [lax.shift_right_logical(root, 1) for root in roots]
    side = [lax.bitwise_and(part, 1) for part in chip]
    line = [lax.shift_right_logical(root, 2) for root in roots]

    parts = streams(rows)
    n_streams = len(parts)
    above_side = lax.bitwise_and(lax.shift_right_logical(index[0, above[0]], 1), 1)

    def piece(q, o):
        lo, n = parts[q % n_streams][1:]
        return pl.ds(pl.multiple_of(o * rows + lo, 8), n)

    def part(q):
        return pl.ds(*parts[q % n_streams][1:])

    def front(q):
        return parts[q % n_streams][0] + PREV * (q // n_streams)

    def candidate(q, o):
        return where(roots[front(q)], sib[1], sib_blk[piece(q, o), :], blk[core, piece(q, o), :])

    def p_copy(q, s):
        f, i = front(q), q * plus + s
        at = f * plus + s
        return remote(ps.at[at, part(q)], pr.at[at, part(q)], p_ssem.at[i], p_rsem.at[i], up)

    def m_copy(q, s):
        f, i = front(q), q * minus + s
        at = f * minus + s
        return remote(ms.at[at, part(q)], mr.at[at, part(q)], m_ssem.at[i], m_rsem.at[i], down)

    def x_copy(q):
        return remote(xs.at[front(q), part(q)], xr.at[front(q), part(q)], x_ssem.at[q], x_rsem.at[q], across)

    def same_copy(q):
        return remote(xs.at[0, part(q)], same_r.at[part(q)], same_ssem.at[q], same_rsem.at[q], below)

    def cross_copy(q):
        return remote(xs.at[0, part(q)], cross_r.at[part(q)], cross_ssem.at[q], cross_rsem.at[q], across_below)

    def ap_copy(q, s):
        at = vb.at[front(q), core, piece(q, (y + ny - s) % ny)]
        return remote(at, at, ap_ssem.at[q * plus + s], ap_rsem.at[q * plus + s], up)

    def ap_wait(q, s):
        at = vb.at[front(q), core, piece(q, (y + ny - 1 - s) % ny)]
        remote(at, at, ap_ssem.at[q * plus + s], ap_rsem.at[q * plus + s], up).wait_recv()

    def am_copy(q, s):
        at = vb.at[front(q), core, piece(q, (y + s) % ny)]
        return remote(at, at, am_ssem.at[q * minus + s], am_rsem.at[q * minus + s], down)

    def am_wait(q, s):
        at = vb.at[front(q), core, piece(q, (y + 1 + s) % ny)]
        remote(at, at, am_ssem.at[q * minus + s], am_rsem.at[q * minus + s], down).wait_recv()

    def c_copy(q, t, o):
        at = vb.at[front(q), core, piece(q, o)]
        return remote(at, at, c_ssem.at[q * ny + t], c_rsem.at[q * ny + t], sib)

    def c_wait(q, t, o):
        at = vb.at[front(q), other, piece(q, o)]
        remote(at, at, c_ssem.at[q * ny + t], c_rsem.at[q * ny + t], sib).wait_recv()

    def slots():
        yield 0, y
        for s in range(plus):
            yield 1 + s, (y + ny - 1 - s) % ny
        for s in range(minus):
            yield 1 + plus + s, (y + 1 + s) % ny

    def z_copy(q):
        f = front(q)
        src, dst = vb.at[f, core, piece(q, y)], vb.at[PREV + f, core, piece(q, y)]
        return remote(src, dst, z_ssem.at[q], z_rsem.at[q], below)

    def select(q, s):
        f = front(q)
        mine = candidate(q, (y + plus - s) % ny)
        if s > 0:
            p_copy(q, s - 1).wait_recv()
            mine = where(chip[f], vec // 2, mine, pr[f * plus + s - 1, part(q), :])
        ps[f * plus + s, part(q), :] = mine
        if s < minus:
            back = candidate(q, (y + ny - minus + s) % ny)
            if s > 0:
                m_copy(q, s - 1).wait_recv()
                back = where(chip[f], vec // 2, back, mr[f * minus + s - 1, part(q), :])
            ms[f * minus + s, part(q), :] = back
        p_copy(q, s).start()
        if s < minus:
            m_copy(q, s).start()

    def swap(q):
        f = front(q)
        p_copy(q, plus - 1).wait_recv()
        m_copy(q, minus - 1).wait_recv()
        got = pr[f * plus + plus - 1, part(q), :]
        for s in range(minus):
            got = where(line[f], (y + 1 + s) % ny, mr[f * minus + minus - 1, part(q), :], got)
        xs[f, part(q), :] = where(chip[f], vec // 2, candidate(q, y), got)
        x_copy(q).start()
        if f == 0:
            same_copy(q).start()
            cross_copy(q).start()

    def begin(q):
        f = front(q)
        if q < n_streams:
            x_copy(q).wait_recv()
            vb[f, core, piece(q, y), :] = where(side[f], half, xs[f, part(q), :], xr[f, part(q), :])
        elif f == PREV:
            same_copy(q - n_streams).wait_recv()
            cross_copy(q - n_streams).wait_recv()
            vb[f, core, piece(q, y), :] = where(above_side, half, same_r[part(q), :], cross_r[part(q), :])
        else:
            z_copy(q - n_streams).wait_recv()
        ap_copy(q, 0).start()
        am_copy(q, 0).start()
        if 0 < f < PREV:
            z_copy(q).start()
        c_copy(q, 0, y).start()

    def gather(q, s):
        ap_wait(q, s)
        if s + 1 < plus:
            ap_copy(q, s + 1).start()
        if s < minus:
            am_wait(q, s)
            if s + 1 < minus:
                am_copy(q, s + 1).start()
        c_copy(q, 1 + s, (y + ny - 1 - s) % ny).start()
        if s < minus:
            c_copy(q, 1 + plus + s, (y + 1 + s) % ny).start()

    def whole(g):
        for q in range(2 * n_streams):
            if front(q) == g:
                for t, o in slots():
                    c_wait(q, t, o)

    delay = {0: 0, 1: 0, 4: 0, 5: 0, 2: 1, 6: 2, 3: 3, 7: 4}

    def tick(t):
        for q, late in delay.items():
            s = t - late - 1
            if s == -1:
                begin(q)
            elif 0 <= s < plus:
                gather(q, s)

    raw.wait_recv()
    for s in range(plus):
        for q in range(n_streams):
            select(q, s)
    for q in range(n_streams):
        swap(q)

    def prepare(f):
        for j in range(2):
            block = vb[f, j, 0:512, :]
            v_h[f, :, j * H : (j + 1) * H], v_l[f, :, j * H : (j + 1) * H] = split(block)
            vt_h[f, j * H : (j + 1) * H, :], vt_l[f, j * H : (j + 1) * H, :] = split(block.T)
        upper = lax.broadcasted_iota(jnp.int32, (H, H), 0) <= lax.broadcasted_iota(jnp.int32, (H, H), 1)
        a = jnp.where(upper, vb[f, 0, 512:640, :], 0.0)
        b = vb[f, 1, 512:640, :]
        c = jnp.where(upper, jnp.concatenate([vb[f, 1, 640:704, :], vb[f, 0, 640:704, :]], axis=0), 0.0)
        zero = jnp.zeros((H, H), F32)
        if f >= PREV:
            place, crossing = offset[f - PREV, above[0]], 3 + (n_row - row) // n_row
        for i, j, part in ((0, 0, a), (0, 1, b), (1, 0, zero), (1, 1, c)):
            at = (f, slice(i * H, (i + 1) * H), slice(j * H, (j + 1) * H))
            s_h[at], s_l[at] = split(where(place, crossing, part, zero) if f >= PREV else part)

    for t in range(plus + 1):
        tick(t)
    for copy in loads:
        copy.wait()
    whole(0)
    prepare(0)
    whole(PREV)
    prepare(PREV)

    def out_copy(c):
        return pltpu.make_async_copy(w.at[c], out.at[:, pl.ds(c * wide, wide)], out_sem.at[c])

    def edge(f, c, k):
        g = PREV + f
        b, t = split(bin_[k]), split(w[c, 0:R, :])
        inner = mm((vt_h[g, :, 0:R], vt_l[g, :, 0:R]), b) + mm((vt_h[g, :, R : 2 * R], vt_l[g, :, R : 2 * R]), t)
        mixed = split(mm((s_h[g], s_l[g]), split(inner)))
        w[c, 0:R, :] = w[c, 0:R, :] - mm((v_h[g, R : 2 * R, :], v_l[g, R : 2 * R, :]), mixed)

    def own(f, c, k):
        place = offset[f, row]
        parts = [w[c, b * R : (b + 1) * R, :] for b in range(4)] + [din[k]]
        window = [parts[3 + i] for i in range(2)]
        for b in (2, 1, 0):
            window = [where(place, b, parts[b + i], window[i]) for i in range(2)]
        inner = mm((vt_h[f], vt_l[f]), split(jnp.concatenate(window, axis=0)))
        mixed = split(mm((s_h[f], s_l[f]), split(inner)))
        pad[...] = mm((v_h[f], v_l[f]), mixed)
        none = jnp.zeros((R, wide), F32)

        def fresh(b):
            lower = where(place, b - 1, pad[R : 2 * R, :], none) if b > 0 else none
            return w[c, b * R : (b + 1) * R, :] - where(place, b, pad[0:R, :], lower)

        top, bottom = fresh(0), fresh(3)

        @pl.when(k < (FRONTS - 1) * NC)
        def _():
            dout[k] = top
            bout[k] = bottom

        w[c, 0:R, :] = top
        w[c, 3 * R : 4 * R, :] = bottom
        for b in (1, 2):
            w[c, b * R : (b + 1) * R, :] = fresh(b)

        @pl.when(k < (FRONTS - 1) * NC)
        def _():
            d_copy(k + NC, dout.at[k]).start()
            b_copy(k + NC, bout.at[k]).start()

        @pl.when(k >= (FRONTS - 1) * NC)
        def _():
            pltpu.make_async_copy(
                w.at[c], out.at[:, pl.ds(pl.multiple_of(c * wide, wide), wide)], out_sem.at[c]
            ).start()

    def step(k, carry):
        @pl.when(k == 1)
        def _():
            tick(plus + 1)

        @pl.when(k == 3)
        def _():
            tick(plus + 2)

        @pl.when(k == 4)
        def _():
            tick(plus + 3)
            for g in (1, PREV + 1):
                whole(g)
                prepare(g)

        @pl.when(k == 6)
        def _():
            tick(plus + 4)

        @pl.when(k == 8)
        def _():
            for g in (2, PREV + 2):
                whole(g)
                prepare(g)

        d_copy(k, dout.at[0]).wait_recv()
        b_copy(k, bout.at[0]).wait_recv()
        f, c = k // NC, k % NC
        edge(f, c, k)
        own(f, c, k)
        return carry

    lax.fori_loop(0, FRONTS * NC, step, 0)

    raw.wait_send()
    for q in range(2 * n_streams):
        if q < n_streams:
            x_copy(q).wait_send()
            if front(q) == 0:
                same_copy(q).wait_send()
                cross_copy(q).wait_send()
            else:
                z_copy(q).wait_send()
            for s in range(plus):
                p_copy(q, s).wait_send()
            for s in range(minus):
                m_copy(q, s).wait_send()
        for s in range(plus):
            ap_copy(q, s).wait_send()
        for s in range(minus):
            am_copy(q, s).wait_send()
        for t, o in slots():
            c_copy(q, t, o).wait_send()
    for k in range(FRONTS * NC):
        d_copy(k, dout.at[0]).wait_send()
        b_copy(k, bout.at[0]).wait_send()
    for c in range(NC):
        out_copy(c).wait()


def solution(mesh):
    n_row, n_vec = mesh.shape["row"], mesh.shape["vec"]
    ny = n_vec // 4
    plus, minus = ny // 2, ny // 2 - 1

    def body(vectors, block_index, block_offset, reflector_vectors, reflector_factors):
        wide = vectors.shape[1] // NC
        steps = FRONTS * NC
        dma = pltpu.SemaphoreType.DMA
        hbm = pl.BlockSpec(memory_space=pltpu.HBM)
        vmem = pltpu.VMEM
        rows = PACK // ny
        return pl.pallas_call(
            functools.partial(kernel, n_row, n_vec),
            out_shape=jax.ShapeDtypeStruct(vectors.shape, F32),
            in_specs=[hbm] * 5,
            out_specs=pl.BlockSpec(memory_space=pl.ANY),
            scratch_shapes=[
                pltpu.SMEM((FRONTS, n_row), jnp.int32),
                pltpu.SMEM((FRONTS, n_row), jnp.int32),
                vmem((NC, 4 * R, wide), F32),
                vmem((NC, R, wide), F32),
                vmem((NC, R, wide), F32),
                vmem((steps, R, wide), F32),
                vmem((steps, R, wide), F32),
                vmem((steps - NC, R, wide), F32),
                vmem((steps - NC, R, wide), F32),
                vmem((2 * R, wide), F32),
                vmem((2, PACK, H), F32),
                vmem((PACK, H), F32),
                vmem((2 * FRONTS, 2, PACK, H), F32),
                vmem((FRONTS * plus, rows, H), F32),
                vmem((FRONTS * plus, rows, H), F32),
                vmem((FRONTS * minus, rows, H), F32),
                vmem((FRONTS * minus, rows, H), F32),
                vmem((FRONTS, rows, H), F32),
                vmem((FRONTS, rows, H), F32),
                vmem((rows, H), F32),
                vmem((rows, H), F32),
                vmem((2 * FRONTS, R, 2 * R), BF16),
                vmem((2 * FRONTS, R, 2 * R), BF16),
                vmem((2 * FRONTS, 2 * R, R), BF16),
                vmem((2 * FRONTS, 2 * R, R), BF16),
                vmem((2 * FRONTS, R, R), BF16),
                vmem((2 * FRONTS, R, R), BF16),
                dma((7 + 3 * NC,)),
                dma((2,)),
                dma((4 * plus,)),
                dma((4 * plus,)),
                dma((4 * minus,)),
                dma((4 * minus,)),
                dma((4,)),
                dma((4,)),
                dma((4,)),
                dma((4,)),
                dma((2,)),
                dma((2,)),
                dma((2,)),
                dma((2,)),
                dma((8 * plus,)),
                dma((8 * plus,)),
                dma((8 * minus,)),
                dma((8 * minus,)),
                dma((8 * ny,)),
                dma((8 * ny,)),
                dma((steps,)),
                dma((steps,)),
                dma((steps,)),
                dma((steps,)),
                dma((NC,)),
            ],
            compiler_params=pltpu.CompilerParams(
                collective_id=0, has_side_effects=True, vmem_limit_bytes=48 * 1024 * 1024
            ),
            name="fronts",
        )(
            *(
                pltpu.with_memory_space_constraint(array, pltpu.HBM)
                for array in (vectors, block_index, block_offset, reflector_vectors, reflector_factors)
            )
        )

    return jax.shard_map(
        body,
        mesh=mesh,
        in_specs=(P("row", "vec"), P(), P(), P("row", "vec", None, None), P("row", "vec", None, None)),
        out_specs=P("row", "vec"),
        check_vma=False,
    )
```

```python
import functools

import jax
import jax.numpy as jnp
from jax import lax
from jax.experimental import pallas as pl
from jax.experimental.pallas import tpu as pltpu
from jax.sharding import PartitionSpec as P

MESH = pl.DeviceIdType.MESH
F32, BF16 = jnp.float32, jnp.bfloat16
FRONTS = 3
PREV = FRONTS
R = 256
H = 128
PACK = 704
NC = 4


def streams(rows):
    cut = (rows // 8 + 1) // 2 * 8
    return ((0, 0, cut), (0, cut, rows - cut), (1, 0, rows), (2, 0, rows))


def split(x):
    high = x.astype(BF16)
    return high, (x - high.astype(F32)).astype(BF16)


def where(value, target, yes, no):
    return jnp.where(jnp.full(yes.shape, value, jnp.int32) == jnp.full(yes.shape, target, jnp.int32), yes, no)


def mm(a, b):
    dot = functools.partial(jnp.dot, preferred_element_type=F32)
    return dot(a[0], b[0]) + (dot(a[0], b[1]) + dot(a[1], b[0]))


def kernel(
    n_row,
    n_vec,
    slab,
    index_hbm,
    offset_hbm,
    v_hbm,
    s_hbm,
    out,
    index,
    offset,
    w,
    first,
    last,
    bin_,
    din,
    dout,
    bout,
    pad,
    blk,
    sib_blk,
    vb,
    ps,
    pr,
    ms,
    mr,
    xs,
    xr,
    same_r,
    cross_r,
    vt_h,
    vt_l,
    v_h,
    v_l,
    s_h,
    s_l,
    in_sem,
    raw_sem,
    p_ssem,
    p_rsem,
    m_ssem,
    m_rsem,
    x_ssem,
    x_rsem,
    z_ssem,
    z_rsem,
    same_ssem,
    same_rsem,
    cross_ssem,
    cross_rsem,
    ap_ssem,
    ap_rsem,
    am_ssem,
    am_rsem,
    c_ssem,
    c_rsem,
    d_ssem,
    d_rsem,
    b_ssem,
    b_rsem,
    out_sem,
):
    ny = n_vec // 4
    plus, minus = ny // 2, ny // 2 - 1
    rows = PACK // ny
    wide = w.shape[2]
    row, vec = lax.axis_index("row"), lax.axis_index("vec")
    y, half, core = vec // 4, (vec // 2) % 2, vec % 2
    up = (row, ((y + 1) % ny) * 4 + vec % 4)
    down = (row, ((y + ny - 1) % ny) * 4 + vec % 4)
    sib = (row, vec + 1 - 2 * core)
    across = (row, vec + 2 - 4 * half)
    below = ((row + 1) % n_row, vec)
    across_below = (below[0], across[1])
    above = ((row + n_row - 1) % n_row, vec)
    across_above = (above[0], across[1])
    other = 1 - core

    def remote(src, dst, ssem, rsem, to):
        return pltpu.make_async_remote_copy(
            src_ref=src, dst_ref=dst, send_sem=ssem, recv_sem=rsem, device_id=to, device_id_type=MESH
        )

    stage = [
        pltpu.make_async_copy(v_hbm.at[0, 0, :, pl.ds(0, H)], blk.at[0, pl.ds(0, 512)], in_sem.at[0]),
        pltpu.make_async_copy(v_hbm.at[0, 0, :, pl.ds(H, H)], blk.at[1, pl.ds(0, 512)], in_sem.at[1]),
        pltpu.make_async_copy(s_hbm.at[0, 0, pl.ds(0, 128), pl.ds(0, H)], blk.at[0, pl.ds(512, 128)], in_sem.at[2]),
        pltpu.make_async_copy(s_hbm.at[0, 0, pl.ds(192, 64), pl.ds(H, H)], blk.at[0, pl.ds(640, 64)], in_sem.at[3]),
        pltpu.make_async_copy(s_hbm.at[0, 0, pl.ds(0, 192), pl.ds(H, H)], blk.at[1, pl.ds(512, 192)], in_sem.at[4]),
        pltpu.make_async_copy(index_hbm, index, in_sem.at[5 + 3 * NC]),
        pltpu.make_async_copy(offset_hbm, offset, in_sem.at[6 + 3 * NC]),
    ]
    firsts = [
        pltpu.make_async_copy(slab.at[pl.ds(0, R), pl.ds(c * wide, wide)], first.at[c], in_sem.at[5 + c])
        for c in range(NC)
    ]
    lasts = [
        pltpu.make_async_copy(slab.at[pl.ds(3 * R, R), pl.ds(c * wide, wide)], last.at[c], in_sem.at[5 + NC + c])
        for c in range(NC)
    ]
    loads = [
        pltpu.make_async_copy(slab.at[:, pl.ds(c * wide, wide)], w.at[c], in_sem.at[5 + 2 * NC + c])
        for c in range(NC)
    ]
    for copy in stage + firsts + lasts + loads:
        copy.start()

    barrier = pltpu.get_barrier_semaphore()
    for to in (up, down, sib, across, below, above, across_below, across_above):
        pl.semaphore_signal(barrier, inc=1, device_id=to, device_id_type=MESH)
    pl.semaphore_wait(barrier, 8)

    for copy in stage:
        copy.wait()
    raw = remote(blk.at[other], sib_blk, raw_sem.at[0], raw_sem.at[1], sib)
    raw.start()

    def d_copy(k, src):
        return remote(src, din.at[k], d_ssem.at[0], d_rsem.at[k], above)

    def b_copy(k, src):
        return remote(src, bin_.at[k], b_ssem.at[0], b_rsem.at[k], below)

    for c in range(NC):
        firsts[c].wait()
        d_copy(c, first.at[c]).start()
        lasts[c].wait()
        b_copy(c, last.at[c]).start()

    roots = [index[f, row] for f in range(FRONTS)]
    chip = [lax.shift_right_logical(root, 1) for root in roots]
    side = [lax.bitwise_and(part, 1) for part in chip]
    line = [lax.shift_right_logical(root, 2) for root in roots]

    parts = streams(rows)
    n_streams = len(parts)
    above_side = lax.bitwise_and(lax.shift_right_logical(index[0, above[0]], 1), 1)

    def piece(q, o):
        lo, n = parts[q % n_streams][1:]
        return pl.ds(pl.multiple_of(o * rows + lo, 8), n)

    def part(q):
        return pl.ds(*parts[q % n_streams][1:])

    def front(q):
        return parts[q % n_streams][0] + PREV * (q // n_streams)

    def candidate(q, o):
        return where(roots[front(q)], sib[1], sib_blk[piece(q, o), :], blk[core, piece(q, o), :])

    def p_copy(q, s):
        f, i = front(q), q * plus + s
        at = f * plus + s
        return remote(ps.at[at, part(q)], pr.at[at, part(q)], p_ssem.at[0], p_rsem.at[i], up)

    def m_copy(q, s):
        f, i = front(q), q * minus + s
        at = f * minus + s
        return remote(ms.at[at, part(q)], mr.at[at, part(q)], m_ssem.at[0], m_rsem.at[i], down)

    def x_copy(q):
        return remote(xs.at[front(q), part(q)], xr.at[front(q), part(q)], x_ssem.at[0], x_rsem.at[q], across)

    def same_copy(q):
        return remote(xs.at[0, part(q)], same_r.at[part(q)], same_ssem.at[q], same_rsem.at[q], below)

    def cross_copy(q):
        return remote(xs.at[0, part(q)], cross_r.at[part(q)], cross_ssem.at[q], cross_rsem.at[q], across_below)

    def ap_copy(q, s):
        at = vb.at[front(q), core, piece(q, (y + ny - s) % ny)]
        return remote(at, at, ap_ssem.at[0], ap_rsem.at[q * plus + s], up)

    def ap_wait(q, s):
        at = vb.at[front(q), core, piece(q, (y + ny - 1 - s) % ny)]
        remote(at, at, ap_ssem.at[0], ap_rsem.at[q * plus + s], up).wait_recv()

    def am_copy(q, s):
        at = vb.at[front(q), core, piece(q, (y + s) % ny)]
        return remote(at, at, am_ssem.at[0], am_rsem.at[q * minus + s], down)

    def am_wait(q, s):
        at = vb.at[front(q), core, piece(q, (y + 1 + s) % ny)]
        remote(at, at, am_ssem.at[0], am_rsem.at[q * minus + s], down).wait_recv()

    def c_copy(q, t, o):
        at = vb.at[front(q), core, piece(q, o)]
        return remote(at, at, c_ssem.at[0], c_rsem.at[front(q)], sib)

    def z_copy(q):
        f = front(q)
        src, dst = vb.at[f, core, piece(q, y)], vb.at[PREV + f, core, piece(q, y)]
        return remote(src, dst, z_ssem.at[q], z_rsem.at[q], below)

    def select(q, s):
        f = front(q)
        mine = candidate(q, (y + plus - s) % ny)
        if s > 0:
            p_copy(q, s - 1).wait_recv()
            mine = where(chip[f], vec // 2, mine, pr[f * plus + s - 1, part(q), :])
        ps[f * plus + s, part(q), :] = mine
        if s < minus:
            back = candidate(q, (y + ny - minus + s) % ny)
            if s > 0:
                m_copy(q, s - 1).wait_recv()
                back = where(chip[f], vec // 2, back, mr[f * minus + s - 1, part(q), :])
            ms[f * minus + s, part(q), :] = back
        p_copy(q, s).start()
        if s < minus:
            m_copy(q, s).start()

    def swap(q):
        f = front(q)
        p_copy(q, plus - 1).wait_recv()
        m_copy(q, minus - 1).wait_recv()
        got = pr[f * plus + plus - 1, part(q), :]
        for s in range(minus):
            got = where(line[f], (y + 1 + s) % ny, mr[f * minus + minus - 1, part(q), :], got)
        xs[f, part(q), :] = where(chip[f], vec // 2, candidate(q, y), got)
        x_copy(q).start()
        if f == 0:
            same_copy(q).start()
            cross_copy(q).start()

    def begin(q):
        f = front(q)
        if q < n_streams:
            x_copy(q).wait_recv()
            vb[f, core, piece(q, y), :] = where(side[f], half, xs[f, part(q), :], xr[f, part(q), :])
        elif f == PREV:
            same_copy(q - n_streams).wait_recv()
            cross_copy(q - n_streams).wait_recv()
            vb[f, core, piece(q, y), :] = where(above_side, half, same_r[part(q), :], cross_r[part(q), :])
        else:
            z_copy(q - n_streams).wait_recv()
        ap_copy(q, 0).start()
        am_copy(q, 0).start()
        if 0 < f < PREV:
            z_copy(q).start()
        c_copy(q, 0, y).start()

    def gather(q, s):
        ap_wait(q, s)
        if s + 1 < plus:
            ap_copy(q, s + 1).start()
        if s < minus:
            am_wait(q, s)
            if s + 1 < minus:
                am_copy(q, s + 1).start()
        c_copy(q, 1 + s, (y + ny - 1 - s) % ny).start()
        if s < minus:
            c_copy(q, 1 + plus + s, (y + 1 + s) % ny).start()

    def whole(g):
        view = vb.at[g, other]
        remote(view, view, c_ssem.at[0], c_rsem.at[g], sib).wait_recv()

    delay = {0: 0, 1: 0, 4: 0, 5: 0, 2: 1, 6: 2, 3: 3, 7: 4}

    def tick(t):
        for q, late in delay.items():
            s = t - late - 1
            if s == -1:
                begin(q)
            elif 0 <= s < plus:
                gather(q, s)

    raw.wait_recv()
    for s in range(plus):
        for q in range(n_streams):
            select(q, s)
    for q in range(n_streams):
        swap(q)

    def prepare(f):
        for j in range(2):
            block = vb[f, j, 0:512, :]
            v_h[f, :, j * H : (j + 1) * H], v_l[f, :, j * H : (j + 1) * H] = split(block)
            vt_h[f, j * H : (j + 1) * H, :], vt_l[f, j * H : (j + 1) * H, :] = split(block.T)
        upper = lax.broadcasted_iota(jnp.int32, (H, H), 0) <= lax.broadcasted_iota(jnp.int32, (H, H), 1)
        a = jnp.where(upper, vb[f, 0, 512:640, :], 0.0)
        b = vb[f, 1, 512:640, :]
        c = jnp.where(upper, jnp.concatenate([vb[f, 1, 640:704, :], vb[f, 0, 640:704, :]], axis=0), 0.0)
        zero = jnp.zeros((H, H), F32)
        if f >= PREV:
            place, crossing = offset[f - PREV, above[0]], 3 + (n_row - row) // n_row
        for i, j, part in ((0, 0, a), (0, 1, b), (1, 0, zero), (1, 1, c)):
            at = (f, slice(i * H, (i + 1) * H), slice(j * H, (j + 1) * H))
            s_h[at], s_l[at] = split(where(place, crossing, part, zero) if f >= PREV else part)

    for t in range(plus + 1):
        tick(t)
    for copy in loads:
        copy.wait()
    whole(0)
    prepare(0)
    whole(PREV)
    prepare(PREV)

    def out_copy(c):
        return pltpu.make_async_copy(w.at[c], out.at[:, pl.ds(c * wide, wide)], out_sem.at[c])

    def edge(f, c, k):
        g = PREV + f
        b, t = split(bin_[k]), split(w[c, 0:R, :])
        inner = mm((vt_h[g, :, 0:R], vt_l[g, :, 0:R]), b) + mm((vt_h[g, :, R : 2 * R], vt_l[g, :, R : 2 * R]), t)
        mixed = split(mm((s_h[g], s_l[g]), split(inner)))
        w[c, 0:R, :] = w[c, 0:R, :] - mm((v_h[g, R : 2 * R, :], v_l[g, R : 2 * R, :]), mixed)

    def own(f, c, k):
        place = offset[f, row]
        parts = [w[c, b * R : (b + 1) * R, :] for b in range(4)] + [din[k]]
        window = [parts[3 + i] for i in range(2)]
        for b in (2, 1, 0):
            window = [where(place, b, parts[b + i], window[i]) for i in range(2)]
        inner = mm((vt_h[f], vt_l[f]), split(jnp.concatenate(window, axis=0)))
        mixed = split(mm((s_h[f], s_l[f]), split(inner)))
        pad[...] = mm((v_h[f], v_l[f]), mixed)
        none = jnp.zeros((R, wide), F32)

        def fresh(b):
            lower = where(place, b - 1, pad[R : 2 * R, :], none) if b > 0 else none
            return w[c, b * R : (b + 1) * R, :] - where(place, b, pad[0:R, :], lower)

        top, bottom = fresh(0), fresh(3)

        @pl.when(k < (FRONTS - 1) * NC)
        def _():
            dout[k] = top
            bout[k] = bottom

        w[c, 0:R, :] = top
        w[c, 3 * R : 4 * R, :] = bottom
        for b in (1, 2):
            w[c, b * R : (b + 1) * R, :] = fresh(b)

        @pl.when(k < (FRONTS - 1) * NC)
        def _():
            d_copy(k + NC, dout.at[k]).start()
            b_copy(k + NC, bout.at[k]).start()

        @pl.when(k >= (FRONTS - 1) * NC)
        def _():
            pltpu.make_async_copy(
                w.at[c], out.at[:, pl.ds(pl.multiple_of(c * wide, wide), wide)], out_sem.at[c]
            ).start()

    def step(k, carry):
        @pl.when(k == 1)
        def _():
            tick(plus + 1)

        @pl.when(k == 3)
        def _():
            tick(plus + 2)

        @pl.when(k == 4)
        def _():
            tick(plus + 3)
            for g in (1, PREV + 1):
                whole(g)
                prepare(g)

        @pl.when(k == 6)
        def _():
            tick(plus + 4)

        @pl.when(k == 8)
        def _():
            for g in (2, PREV + 2):
                whole(g)
                prepare(g)

        d_copy(k, dout.at[0]).wait_recv()
        b_copy(k, bout.at[0]).wait_recv()
        f, c = k // NC, k % NC
        edge(f, c, k)
        own(f, c, k)
        return carry

    lax.fori_loop(0, FRONTS * NC, step, 0)

    raw.wait_send()
    def sent(view, ssem, rsem, to):
        remote(view, view, ssem, rsem, to).wait_send()

    for q in range(n_streams):
        if front(q) == 0:
            same_copy(q).wait_send()
            cross_copy(q).wait_send()
        else:
            z_copy(q).wait_send()
    sent(xs, x_ssem.at[0], x_rsem.at[0], across)
    sent(ps, p_ssem.at[0], p_rsem.at[0], up)
    sent(ms, m_ssem.at[0], m_rsem.at[0], down)
    sent(vb.at[:, core, pl.ds(0, plus * rows)], ap_ssem.at[0], ap_rsem.at[0], up)
    sent(vb.at[:, core, pl.ds(0, minus * rows)], am_ssem.at[0], am_rsem.at[0], down)
    sent(vb.at[:, core], c_ssem.at[0], c_rsem.at[0], sib)
    sent(din, d_ssem.at[0], d_rsem.at[0], above)
    sent(bin_, b_ssem.at[0], b_rsem.at[0], below)
    for c in range(NC):
        out_copy(c).wait()


def solution(mesh):
    n_row, n_vec = mesh.shape["row"], mesh.shape["vec"]
    ny = n_vec // 4
    plus, minus = ny // 2, ny // 2 - 1

    def body(vectors, block_index, block_offset, reflector_vectors, reflector_factors):
        wide = vectors.shape[1] // NC
        steps = FRONTS * NC
        dma = pltpu.SemaphoreType.DMA
        hbm = pl.BlockSpec(memory_space=pltpu.HBM)
        vmem = pltpu.VMEM
        rows = PACK // ny
        return pl.pallas_call(
            functools.partial(kernel, n_row, n_vec),
            out_shape=jax.ShapeDtypeStruct(vectors.shape, F32),
            in_specs=[hbm] * 5,
            out_specs=pl.BlockSpec(memory_space=pl.ANY),
            scratch_shapes=[
                pltpu.SMEM((FRONTS, n_row), jnp.int32),
                pltpu.SMEM((FRONTS, n_row), jnp.int32),
                vmem((NC, 4 * R, wide), F32),
                vmem((NC, R, wide), F32),
                vmem((NC, R, wide), F32),
                vmem((steps, R, wide), F32),
                vmem((steps, R, wide), F32),
                vmem((steps - NC, R, wide), F32),
                vmem((steps - NC, R, wide), F32),
                vmem((2 * R, wide), F32),
                vmem((2, PACK, H), F32),
                vmem((PACK, H), F32),
                vmem((2 * FRONTS, 2, PACK, H), F32),
                vmem((FRONTS * plus, rows, H), F32),
                vmem((FRONTS * plus, rows, H), F32),
                vmem((FRONTS * minus, rows, H), F32),
                vmem((FRONTS * minus, rows, H), F32),
                vmem((FRONTS, rows, H), F32),
                vmem((FRONTS, rows, H), F32),
                vmem((rows, H), F32),
                vmem((rows, H), F32),
                vmem((2 * FRONTS, R, 2 * R), BF16),
                vmem((2 * FRONTS, R, 2 * R), BF16),
                vmem((2 * FRONTS, 2 * R, R), BF16),
                vmem((2 * FRONTS, 2 * R, R), BF16),
                vmem((2 * FRONTS, R, R), BF16),
                vmem((2 * FRONTS, R, R), BF16),
                dma((7 + 3 * NC,)),
                dma((2,)),
                dma((1,)),
                dma((4 * plus,)),
                dma((1,)),
                dma((4 * minus,)),
                dma((1,)),
                dma((4,)),
                dma((4,)),
                dma((4,)),
                dma((2,)),
                dma((2,)),
                dma((2,)),
                dma((2,)),
                dma((1,)),
                dma((8 * plus,)),
                dma((1,)),
                dma((8 * minus,)),
                dma((1,)),
                dma((2 * FRONTS,)),
                dma((1,)),
                dma((steps,)),
                dma((1,)),
                dma((steps,)),
                dma((NC,)),
            ],
            compiler_params=pltpu.CompilerParams(
                collective_id=0, has_side_effects=True, vmem_limit_bytes=48 * 1024 * 1024
            ),
            name="fronts",
        )(
            *(
                pltpu.with_memory_space_constraint(array, pltpu.HBM)
                for array in (vectors, block_index, block_offset, reflector_vectors, reflector_factors)
            )
        )

    return jax.shard_map(
        body,
        mesh=mesh,
        in_specs=(P("row", "vec"), P(), P(), P("row", "vec", None, None), P("row", "vec", None, None)),
        out_specs=P("row", "vec"),
        check_vma=False,
    )
```
